32 devices in a mesh: ex: 8 (over y, x, core), co: 4 (over z).
Axes of the slice: x: 2, y: 2, z: 4, core: 2. Of those that a mesh axis runs over, the one named last changes fastest.
Arguments:
- train_grads: float32 [8192, 32768], P('ex', 'co')
- queries: float32 [1024, 32768], P('ex', 'co'), may hold values from -6 to 6
- module_ids: int32 [8], replicated, may hold values from 0 to 223
- module_scale: float32 [224], replicated, may hold values from 0.3 to 3
- example_ids: int32 [8192], P('ex'), may hold values from 0 to 8191, as said below
Outputs:
- influence: float32 [1024, 8192], P('co', 'ex')
The draws below stay inside these ranges and needn't reach their ends.
Inputs may be any that keep to these rules, and one draw needn't show every extreme that they name: `example_ids`: the examples of block s of 1024 rows carry the ids s * 1024 to (s + 1) * 1024 - 1, each once.
All inputs are finite; a program needn't handle non-finite values.
Results may differ from the reference program's by a relative error of at most 0.00008.
Values sent between devices are 32-bit elements; how exact they have to be, the bound alone decides.
A program may use at most 128 MiB of HBM per device.

```python
import math
import jax
import jax.numpy as jnp
from jax import lax

PROJ = 4096
TOTAL_MODS = 224
MODS = 8
E_DEV = 1024
QUERIES = 1024
COORD = 32768
EXAMPLES = 8192


def draw_train_grads(key, part):
    key_row, key_col, key_main = jax.random.split(key, 3)
    row_scale = jnp.exp(jax.random.uniform(key_row, (EXAMPLES, 1), jnp.float32) * jnp.log(10.0))
    col_scale = jnp.exp(jax.random.uniform(key_col, (1, COORD), jnp.float32) * jnp.log(10.0))
    growth = (jnp.arange(COORD, dtype=jnp.float32) / COORD)[None, :]
    growth = jnp.exp(growth * jnp.log(3.0))
    entries = jax.random.normal(key_main, (EXAMPLES, COORD), jnp.float32)
    return (entries * row_scale * col_scale * growth / jnp.sqrt(jnp.float32(COORD))).astype(jnp.float32)


def shuffle_block(block_key):
    return jax.random.permutation(block_key, E_DEV)


def draw_example_ids(key, part):
    shards = EXAMPLES // E_DEV
    shard_keys = jax.random.split(jax.random.fold_in(key, 7), shards)
    shuffled = jax.vmap(shuffle_block)(shard_keys).astype(jnp.int32)
    offsets = (jnp.arange(shards, dtype=jnp.int32) * E_DEV)[:, None]
    return (shuffled + offsets).reshape(-1).astype(jnp.int32)


def place_ends(drawn, stream_key, least, high):
    extent = drawn.shape
    spot = [jax.random.randint(jax.random.fold_in(stream_key, axis), (), 0, extent[axis]) for axis in range(len(extent))]
    drawn = drawn.at[tuple(spot)].set(least)
    longest = extent.index(max(extent))
    spot[longest] = (spot[longest] + 1) % extent[longest]
    return drawn.at[tuple(spot)].set(high)


def with_spikes(values, key, source, target, blocks, factor):
    def block_of(dim):
        return (jnp.arange(values.shape[dim]) // (values.shape[dim] // blocks)).reshape((-1,) + (1,) * (values.ndim - 1 - dim))

    near = jax.random.permutation(key, blocks)[block_of(target)]
    second = (block_of(target) + blocks // 2) % blocks
    return jnp.where((block_of(source) == near) | (block_of(source) == second), factor * values, values)


def levels(stream_key, dims, cuts, low, largest):
    factor_of, own = 1.0, jax.random.fold_in(stream_key, 6)
    for dim, parts in cuts:
        draws = jnp.exp(jax.random.uniform(jax.random.fold_in(own, dim), (parts,), jnp.float32, low / len(cuts), largest / len(cuts)))
        factor_of = factor_of * jnp.repeat(draws, dims[dim] // parts).reshape([-1 if axis == dim else 1 for axis in range(len(dims))])
    return factor_of


def heavy_noise(stream_key, dims, width, bound, cuts, heavy, kind=jnp.bfloat16):
    array = width * jax.random.normal(stream_key, dims, jnp.float32)
    if cuts:
        array = array * levels(stream_key, dims, cuts, -0.22, 0.18)
    return jnp.clip(with_spikes(array, jax.random.fold_in(stream_key, 3), *heavy), -bound, bound).astype(kind)


def setup_inputs(seed: int = 0) -> dict:
    splits = jax.random.split(jax.random.key(seed), 6)
    return {
        "train_grads": draw_train_grads(jax.random.fold_in(splits[5], 71), 0),
        "queries": heavy_noise(splits[1], (QUERIES, COORD), 1.0, 6.0, ((0, 8), (1, 4)), (1, 0, 8, 2.0), jnp.float32),
        "module_ids": place_ends(jax.random.randint(splits[2], (MODS,), 0, TOTAL_MODS), jax.random.fold_in(splits[2], 1), 0, TOTAL_MODS - 1).astype(jnp.int32),
        "module_scale": jnp.clip(jnp.exp(jax.random.uniform(splits[3], (TOTAL_MODS,), jnp.float32, math.log(0.3), math.log(3.0))), 0.3, 3.0),
        "example_ids": draw_example_ids(jax.random.fold_in(splits[5], 71), 0),
    }


epsilon = 1e-06

def reference(train_grads, queries, module_ids, module_scale, example_ids):
    table_index = lax.iota(jnp.int32, module_scale.shape[0])
    picked = lax.optimization_barrier(jnp.sum(jnp.where(module_ids[:, None] == table_index[None, :], module_scale[None, :], jnp.zeros((), module_scale.dtype)), axis=1))
    position = lax.iota(jnp.int32, COORD)
    coord_scale = picked[(position // PROJ).astype(jnp.int32)]
    scaled = queries * coord_scale[None, :]
    squares = lax.optimization_barrier(jnp.sum(train_grads * train_grads, axis=1))
    inverse_norm = lax.rsqrt(squares + epsilon)
    raw_scores = lax.dot_general(scaled, train_grads, (((1,), (1,)), ((), ())), precision=lax.Precision.HIGHEST, preferred_element_type=jnp.float32)
    normed = raw_scores * inverse_norm[None, :]
    return jnp.zeros_like(normed).at[:, example_ids].set(normed)
```

```python
import functools

import jax
import jax.numpy as jnp
from jax import lax
from jax.experimental import pallas as pl
from jax.experimental.pallas import tpu as pltpu
from jax.sharding import PartitionSpec as P

PROJ = 4096
MESH = pl.DeviceIdType.MESH
PIECES = 8
LEAD = 2
CONTRACT_LAST = (((1,), (1,)), ((), ()))

epsilon = 1e-06


def kernel(n_ex, n_co, pieces, q_ref, g_ref, scale_ref, out_ref, buf,
           ghi, glo, fresh, stage, split, part, got, sq_own, sq_got,
           ring_send, ring_recv, sib_send, sib_recv, part_send, part_recv, sq_send, sq_recv, load_sem):
    chips = n_ex // 2
    half = chips // 2
    ex = lax.axis_index("ex")
    co = lax.axis_index("co")
    core = ex % 2

    def snake(pos):
        upper = pos // half
        return pos * (1 - upper) + upper * (half + chips - 1 - pos)

    pos = snake(ex // 2)

    def device_at(step):
        return snake((pos + step + chips) % chips) * 2 + core

    right = device_at(1)
    left = device_at(-1)
    sibling = ex + 1 - 2 * core
    rows = q_ref.shape[0] // pieces
    width = q_ref.shape[1]
    mid = width // 2
    examples = g_ref.shape[0]
    owned = (n_ex // n_co) * rows

    barrier = pltpu.get_barrier_semaphore()
    for other in (right, left, sibling):
        pl.semaphore_signal(barrier, inc=1, device_id={"ex": other}, device_id_type=MESH)
    for k in range(1, n_co):
        pl.semaphore_signal(barrier, inc=1, device_id={"co": (co + k) % n_co}, device_id_type=MESH)
    pl.semaphore_wait(barrier, 3 + n_co - 1)

    def own_rows(s):
        return q_ref.at[pl.ds(pl.multiple_of(s * rows, rows), rows)]

    def ring_copy(way, d, s, arriving):
        back = d if arriving else d - 1
        origin = device_at(-back if way == 0 else back)
        if d == half and half > 1:
            span = pl.ds(way * mid, mid)
        else:
            span = pl.ds(0, width)
        if d == 1 and not arriving:
            src = own_rows(s)
        else:
            src = buf.at[s, origin, :, span]
        return pltpu.make_async_remote_copy(
            src_ref=src,
            dst_ref=buf.at[s, origin, :, span],
            send_sem=ring_send.at[way, d - 1, s],
            recv_sem=ring_recv.at[way, d - 1, s],
            device_id={"ex": right if way == 0 else left},
            device_id_type=MESH,
        )

    def sibling_copy(off, s, arriving):
        origin = device_at(off)
        if arriving:
            origin = origin + 1 - 2 * core
        src = own_rows(s) if off == 0 and not arriving else buf.at[s, origin]
        return pltpu.make_async_remote_copy(
            src_ref=src,
            dst_ref=buf.at[s, origin],
            send_sem=sib_send.at[off, s],
            recv_sem=sib_recv.at[off, s],
            device_id={"ex": sibling},
            device_id_type=MESH,
        )

    block = 256
    blocks = examples // block

    def part_copy(k, s, b):
        owner = (co + k) % n_co
        cols = pl.ds(pl.multiple_of(b * block, block), block)
        return pltpu.make_async_remote_copy(
            src_ref=part.at[s, pl.ds(pl.multiple_of(owner * owned, owned), owned), cols],
            dst_ref=got.at[k - 1, s, :, cols],
            send_sem=part_send.at[k - 1, s, b],
            recv_sem=part_recv.at[k - 1, s, b],
            device_id={"co": owner},
            device_id_type=MESH,
        )

    def sq_copy(k):
        return pltpu.make_async_remote_copy(
            src_ref=sq_own,
            dst_ref=sq_got.at[k - 1],
            send_sem=sq_send.at[k - 1],
            recv_sem=sq_recv.at[k - 1],
            device_id={"co": (co + k) % n_co},
            device_id_type=MESH,
        )

    def send_own(s):
        ring_copy(0, 1, s, False).start()
        ring_copy(1, 1, s, False).start()
        sibling_copy(0, s, False).start()

    for s in range(min(LEAD, pieces)):
        send_own(s)

    def relay(t):
        for d in range(1, half + 1):
            s = t - (d - 1)

            @pl.when((s >= 0) & (s < pieces))
            def _():
                ring_copy(0, d, s, True).wait_recv()
                if d < half:
                    ring_copy(0, d + 1, s, False).start()
                ring_copy(1, d, s, True).wait_recv()
                if d < half:
                    ring_copy(1, d + 1, s, False).start()
                if d == 1:
                    @pl.when(s + LEAD < pieces)
                    def _():
                        send_own(s + LEAD)
                sibling_copy(chips - d, s, False).start()
                if d < half:
                    sibling_copy(d, s, False).start()

    tile = fresh.shape[1]
    tiles = examples // tile
    strip = min(512, width)

    def g_load(i):
        slot = i % 2
        return pltpu.make_async_copy(
            g_ref.at[pl.ds(pl.multiple_of(i * tile, tile), tile)],
            fresh.at[slot],
            load_sem.at[slot],
        )

    g_load(0).start()

    def split_tile(i, sums):
        @pl.when(i + 1 < tiles)
        def _():
            g_load(i + 1).start()

        @pl.when(i == tiles // 2)
        def _():
            relay(0)

        g_load(i).wait()
        slot = i % 2
        dest = pl.multiple_of(i * tile, tile)

        def split_strip(j, total):
            col = pl.ds(pl.multiple_of(j * strip, strip), strip)
            x = fresh[slot, :, col]
            hi = x.astype(jnp.bfloat16)
            ghi[pl.ds(dest, tile), col] = hi
            glo[pl.ds(dest, tile), col] = (x - hi.astype(jnp.float32)).astype(jnp.bfloat16)
            xx = x * x
            for lane in range(0, strip, 128):
                total = total + xx[:, lane:lane + 128]
            return total

        total = lax.fori_loop(0, width // strip, split_strip, jnp.zeros((tile, 128), jnp.float32))
        row = jnp.sum(total.T, axis=0, keepdims=True)
        sq_own[:, pl.ds(dest, tile)] = jnp.broadcast_to(row, (8, tile))
        return sums

    lax.fori_loop(0, tiles, split_tile, 0)
    for k in range(1, n_co):
        sq_copy(k).start()

    depth = min(8192, width)
    count = n_ex * rows

    def load(off, side, s):
        origin = device_at(off)
        if side:
            origin = origin + 1 - 2 * core
        src = own_rows(s) if off == 0 and not side else buf.at[s, origin]
        return pltpu.make_async_copy(
            src,
            stage.at[pl.ds(pl.multiple_of(origin * rows, rows), rows)],
            load_sem.at[2 + off * 2 + side],
        )

    def compute(s):
        for off in range(chips):
            load(off, 0, s).start()
        for off in range(chips):
            sibling_copy(off, s, True).wait_recv()
            load(off, 1, s).start()
        for off in range(chips):
            load(off, 0, s).wait()
            load(off, 1, s).wait()

        def split_queries(j, c):
            col = pl.ds(pl.multiple_of(j * strip, strip), strip)
            x = stage[:, col] * scale_ref[:, col]
            hi = x.astype(jnp.bfloat16)
            split[pl.ds(0, count), col] = hi
            split[pl.ds(count, count), col] = (x - hi.astype(jnp.float32)).astype(jnp.bfloat16)
            return c

        lax.fori_loop(0, width // strip, split_queries, 0)

        def block_scores(b, c):
            ex_rows = pl.ds(pl.multiple_of(b * block, block), block)

            def deepen(j, acc):
                col = pl.ds(pl.multiple_of(j * depth, depth), depth)
                dot = functools.partial(
                    lax.dot_general, dimension_numbers=CONTRACT_LAST, preferred_element_type=jnp.float32
                )
                both = dot(split[:, col], ghi[ex_rows, col])
                small = both[count:] + dot(split[:count, col], glo[ex_rows, col])
                return acc + (small + both[:count])

            acc = lax.fori_loop(0, width // depth, deepen, jnp.zeros((count, block), jnp.float32))
            part[s, :, ex_rows] = acc
            for k in range(1, n_co):
                part_copy(k, s, b).start()
            return c

        lax.fori_loop(0, blocks, block_scores, 0)

    def step(t, c):
        @pl.when(t > 0)
        def _():
            relay(t)

        s = t - (half - 1)

        @pl.when((s >= 0) & (s < pieces))
        def _():
            compute(s)

        return c

    lax.fori_loop(0, pieces + half - 1, step, 0)

    for k in range(1, n_co):
        sq_copy(k).wait_recv()
    squares = sq_own[...]
    for k in range(1, n_co):
        squares = squares + sq_got[k - 1]
    inverse_norm = lax.rsqrt(squares[0:1] + epsilon)

    def finish(s, c):
        for k in range(1, n_co):
            for b in range(blocks):
                part_copy(k, s, b).wait_recv()
        total = part[s, pl.ds(pl.multiple_of(co * owned, owned), owned)]
        for k in range(1, n_co):
            total = total + got[k - 1, s]
        total = total * inverse_norm
        for i in range(n_ex // n_co):
            at = pl.multiple_of(i * rows * pieces + s * rows, rows)
            out_ref[pl.ds(at, rows), :] = total[i * rows:(i + 1) * rows]
        return c

    lax.fori_loop(0, pieces, finish, 0)

    def drain(s, c):
        for way in range(2):
            for d in range(1, half + 1):
                ring_copy(way, d, s, False).wait_send()
        for off in range(chips):
            sibling_copy(off, s, False).wait_send()
        for k in range(1, n_co):
            for b in range(blocks):
                part_copy(k, s, b).wait_send()
        return c

    lax.fori_loop(0, pieces, drain, 0)
    for k in range(1, n_co):
        sq_copy(k).wait_send()


def shards(n_ex, n_co, train_grads, queries, module_ids, module_scale, example_ids):
    examples, width = train_grads.shape
    position = lax.axis_index("co") * width + lax.iota(jnp.int32, width)
    table_index = lax.iota(jnp.int32, module_scale.shape[0])
    picked = jnp.sum(
        jnp.where(module_ids[:, None] == table_index[None, :], module_scale[None, :], 0.0), axis=1
    )
    window_index = lax.iota(jnp.int32, module_ids.shape[0])
    coord_scale = jnp.sum(
        jnp.where((position // PROJ)[:, None] == window_index[None, :], picked[None, :], 0.0), axis=1
    )

    chips = n_ex // 2
    pieces = min(PIECES, queries.shape[0] // 8)
    rows = queries.shape[0] // pieces
    count = n_ex * rows
    owned = (n_ex // n_co) * rows
    f32, bf16 = jnp.float32, jnp.bfloat16
    dma = pltpu.SemaphoreType.DMA
    normed, _ = pl.pallas_call(
        functools.partial(kernel, n_ex, n_co, pieces),
        out_shape=(
            jax.ShapeDtypeStruct((owned * pieces, examples), f32),
            jax.ShapeDtypeStruct((pieces, n_ex, rows, width), f32),
        ),
        in_specs=[
            pl.BlockSpec(memory_space=pl.ANY),
            pl.BlockSpec(memory_space=pl.ANY),
            pl.BlockSpec(memory_space=pltpu.VMEM),
        ],
        out_specs=(pl.BlockSpec(memory_space=pltpu.VMEM), pl.BlockSpec(memory_space=pl.ANY)),
        scratch_shapes=[
            pltpu.VMEM((examples, width), bf16),
            pltpu.VMEM((examples, width), bf16),
            pltpu.VMEM((2, min(128, examples), width), f32),
            pltpu.VMEM((count, width), f32),
            pltpu.VMEM((2 * count, width), bf16),
            pltpu.VMEM((pieces, count, examples), f32),
            pltpu.VMEM((n_co - 1, pieces, owned, examples), f32),
            pltpu.VMEM((8, examples), f32),
            pltpu.VMEM((n_co - 1, 8, examples), f32),
            dma((2, chips // 2, pieces)),
            dma((2, chips // 2, pieces)),
            dma((chips, pieces)),
            dma((chips, pieces)),
            dma((n_co - 1, pieces, examples // 256)),
            dma((n_co - 1, pieces, examples // 256)),
            dma((n_co - 1,)),
            dma((n_co - 1,)),
            dma((2 + n_ex,)),
        ],
        compiler_params=pltpu.CompilerParams(
            collective_id=0, has_side_effects=True, vmem_limit_bytes=67043328
        ),
    )(queries, train_grads, coord_scale[None, :])

    local_ids = example_ids - lax.axis_index("ex") * examples
    place = (local_ids[:, None] == lax.iota(jnp.int32, examples)[None, :]).astype(f32)
    return lax.dot_general(
        normed, place, (((1,), (0,)), ((), ())), precision=lax.Precision.HIGH, preferred_element_type=f32
    )


LEAD2 = 4


def plane_kernel(n_ex, n_co, ids_ref, table_ref, q_ref, g_ref, cols_ref, out_ref, buf,
                 ghi, glo, stage, split, part, got, tail_part, tail_got, place, sq_own, sq_got,
                 own_send, own_recv, rel_send, rel_recv, sib_send, sib_recv,
                 part_send, part_recv, tail_send, tail_recv, sq_send, sq_recv, load_sem, g_sem):
    ex = lax.axis_index("ex")
    co = lax.axis_index("co")
    core = ex % 2
    chip = ex // 2
    cx = chip % 2
    cy = chip // 2
    rows = 8
    pieces = q_ref.shape[0] // rows
    width = q_ref.shape[1]
    mid = width // 2
    examples = g_ref.shape[0]
    per_pass = 2 * rows
    count = n_ex * per_pass
    owned = 2 * per_pass
    passes = pieces // 2
    tail_rows = 2 * LEAD2 * rows

    def chip_at(x):
        fx = cx if x % 2 == 0 else 1 - cx
        fy = cy if x < 2 else 1 - cy
        return fy * 2 + fx

    diag = chip_at(3)
    sibling = ex + 1 - 2 * core
    near = [chip_at(1) * 2 + core, chip_at(2) * 2 + core]

    def origin(x, side):
        return chip_at(x) * 2 + (core if side == 0 else 1 - core)

    barrier = pltpu.get_barrier_semaphore()
    for other in (near[0], near[1], sibling):
        pl.semaphore_signal(barrier, inc=1, device_id={"ex": other}, device_id_type=MESH)
    for k in range(1, n_co):
        pl.semaphore_signal(barrier, inc=1, device_id={"co": (co + k) % n_co}, device_id_type=MESH)
    pl.semaphore_wait(barrier, 3 + n_co - 1)

    def own_rows(p):
        return q_ref.at[pl.ds(pl.multiple_of(p * rows, rows), rows)]

    def own_copy(way, p, arriving):
        src = chip_at(way + 1) * 2 + core if arriving else ex
        return pltpu.make_async_remote_copy(
            src_ref=own_rows(p),
            dst_ref=buf.at[p, src],
            send_sem=own_send.at[way, p],
            recv_sem=own_recv.at[way, p],
            device_id={"ex": near[way]},
            device_id_type=MESH,
        )

    def relay_copy(way, p, arriving):
        src = origin(3, 0) if arriving else near[1 - way]
        span = pl.ds(way * mid, mid)
        return pltpu.make_async_remote_copy(
            src_ref=buf.at[p, src, :, span],
            dst_ref=buf.at[p, src, :, span],
            send_sem=rel_send.at[way, p],
            recv_sem=rel_recv.at[way, p],
            device_id={"ex": near[way]},
            device_id_type=MESH,
        )

    def sib_copy(x, p, arriving):
        src = origin(x, 1 if arriving else 0)
        return pltpu.make_async_remote_copy(
            src_ref=own_rows(p) if x == 0 else buf.at[p, src],
            dst_ref=buf.at[p, src],
            send_sem=sib_send.at[x, p],
            recv_sem=sib_recv.at[x, p],
            device_id={"ex": sibling},
            device_id_type=MESH,
        )

    block = 256
    blocks = examples // block

    def block_cols(b):
        return pl.ds(pl.multiple_of(b * block, block), block)

    def part_copy(k, u, b):
        owner = (co + k) % n_co
        return pltpu.make_async_remote_copy(
            src_ref=part.at[u, pl.ds(pl.multiple_of(owner * owned, owned), owned), block_cols(b)],
            dst_ref=got.at[k - 1, u, :, block_cols(b)],
            send_sem=part_send.at[k - 1, u, b],
            recv_sem=part_recv.at[k - 1, u, b],
            device_id={"co": owner},
            device_id_type=MESH,
        )

    above = (co > diag).astype(jnp.int32)
    depth = co + above * (n_co - 1 - 2 * co)

    def tail_copy(slot, b):
        return pltpu.make_async_remote_copy(
            src_ref=tail_part.at[:, block_cols(b)],
            dst_ref=tail_got.at[slot, :, block_cols(b)],
            send_sem=tail_send.at[b],
            recv_sem=tail_recv.at[slot, b],
            device_id={"co": (co + 1 - 2 * slot + n_co) % n_co},
            device_id_type=MESH,
        )

    def sq_copy(k):
        return pltpu.make_async_remote_copy(
            src_ref=sq_own,
            dst_ref=sq_got.at[k - 1],
            send_sem=sq_send.at[k - 1],
            recv_sem=sq_recv.at[k - 1],
            device_id={"co": (co + k) % n_co},
            device_id_type=MESH,
        )

    def send_own(p):
        own_copy(0, p, False).start()
        own_copy(1, p, False).start()
        sib_copy(0, p, False).start()

    for p in range(LEAD2):
        send_own(p)

    def forward(p):
        own_copy(1, p, True).wait_recv()
        relay_copy(0, p, False).start()
        own_copy(0, p, True).wait_recv()
        relay_copy(1, p, False).start()

        @pl.when(p + LEAD2 < pieces)
        def _():
            send_own(p + LEAD2)

        sib_copy(1, p, False).start()
        sib_copy(2, p, False).start()

    def share_diag(p):
        relay_copy(0, p, True).wait_recv()
        relay_copy(1, p, True).wait_recv()
        sib_copy(3, p, False).start()

    tile = stage.shape[1]
    tiles = examples // tile
    strip = min(512, width)

    def g_load(i):
        return pltpu.make_async_copy(
            g_ref.at[pl.ds(pl.multiple_of(i * tile, tile), tile)], stage.at[i % 2], g_sem.at[i % 2]
        )

    g_load(0).start()

    local = cols_ref[...] - ex * examples
    for i in range(examples // 128):
        spot = lax.broadcasted_iota(jnp.int32, (128, examples), 0) + i * 128
        hot = (spot == local).astype(jnp.float32).astype(jnp.bfloat16)
        place[:, i * 128:(i + 1) * 128] = hot.T

    def split_tile(i, c):
        @pl.when(i + 1 < tiles)
        def _():
            g_load(i + 1).start()

        @pl.when(i == tiles - 2)
        def _():
            forward(0)

        g_load(i).wait()
        slot = i % 2
        dest = pl.ds(pl.multiple_of(i * tile, tile), tile)

        def split_strip(j, total):
            col = pl.ds(pl.multiple_of(j * strip, strip), strip)
            x = stage[slot, :, col]
            hi = x.astype(jnp.bfloat16)
            ghi[col, dest] = hi.T
            glo[col, dest] = (x - hi.astype(jnp.float32)).astype(jnp.bfloat16).T
            xx = x * x
            for lane in range(0, strip, 128):
                total = total + xx[:, lane:lane + 128]
            return total

        total = lax.fori_loop(0, width // strip, split_strip, jnp.zeros((tile, 128), jnp.float32))
        row = jnp.sum(total.T, axis=0, keepdims=True)
        sq_own[:, dest] = jnp.broadcast_to(row, (8, tile))
        return c

    lax.fori_loop(0, tiles, split_tile, 0)
    for k in range(1, n_co):
        sq_copy(k).start()

    def load(x, side, p, slot, row, sem):
        src = own_rows(p) if x == 0 and side == 0 else buf.at[p, origin(x, side)]
        return pltpu.make_async_copy(src, stage.at[slot, pl.ds(pl.multiple_of(row, rows), rows)], sem)

    def pass_load(x, side, j, u):
        p = 2 * u + j - (LEAD2 if x == 3 else 0)
        return load(x, side, p, u % 2, origin(x, side) * per_pass + j * rows, load_sem.at[x, side, j])

    def split_queries(slot, m):
        def body(j, c):
            col = pl.ds(pl.multiple_of(j * strip, strip), strip)
            scale = table_ref[ids_ref[(co * width + j * strip) // PROJ]]
            x = stage[slot, :m, col] * scale
            hi = x.astype(jnp.bfloat16)
            split[pl.ds(0, m), col] = hi
            split[pl.ds(m, m), col] = (x - hi.astype(jnp.float32)).astype(jnp.bfloat16)
            return c

        lax.fori_loop(0, width // strip, body, 0)

    def scores(m, b):
        cols = block_cols(b)
        both = jnp.dot(split[:2 * m, :], ghi[:, cols], preferred_element_type=jnp.float32)
        small = both[m:] + jnp.dot(split[:m, :], glo[:, cols], preferred_element_type=jnp.float32)
        return small + both[:m]

    def settle(total):
        squares = sq_own[...]
        for k in range(1, n_co):
            squares = squares + sq_got[k - 1]
        total = total * lax.rsqrt(squares[0:1] + epsilon)
        m = total.shape[0]
        hi = total.astype(jnp.bfloat16)
        rest = total - hi.astype(jnp.float32)
        half = rest.astype(jnp.bfloat16)
        last = (rest - half.astype(jnp.float32)).astype(jnp.bfloat16)
        three = jnp.concatenate([hi, half, last], axis=0)
        moved = jnp.dot(three, place[...], preferred_element_type=jnp.float32)
        return moved[:m] + (moved[m:2 * m] + moved[2 * m:])

    def finish(u):
        for k in range(1, n_co):
            for b in range(blocks):
                part_copy(k, u, b).wait_recv()
        lag = (co == diag).astype(jnp.int32) * LEAD2
        first = 2 * u - lag

        @pl.when(first >= 0)
        def _():
            total = part[u, pl.ds(pl.multiple_of(co * owned, owned), owned)]
            for k in range(1, n_co):
                total = total + got[k - 1, u]
            moved = settle(total)
            for i in range(2):
                at = pl.multiple_of(i * pieces * rows + first * rows, rows)
                out_ref[pl.ds(at, per_pass), :] = moved[i * per_pass:(i + 1) * per_pass]

    tail_first = pieces - LEAD2

    def tail_load(i, side):
        where = (core if side == 0 else 1 - core) * (LEAD2 * rows) + i * rows
        return load(3, side, tail_first + i, passes % 2, where, load_sem.at[i, side, 0])

    def one_pass(u, c):
        @pl.when(u > 0)
        def _():
            forward(2 * u)

        forward(2 * u + 1)

        @pl.when(u >= LEAD2 // 2)
        def _():
            for j in range(2):
                share_diag(2 * u + j - LEAD2)

        for x in range(3):
            for j in range(2):
                pass_load(x, 0, j, u).start()

        @pl.when(u >= LEAD2 // 2)
        def _():
            for j in range(2):
                pass_load(3, 0, j, u).start()

        for x in range(3):
            for j in range(2):
                sib_copy(x, 2 * u + j, True).wait_recv()
                pass_load(x, 1, j, u).start()

        @pl.when(u >= LEAD2 // 2)
        def _():
            for j in range(2):
                sib_copy(3, 2 * u + j - LEAD2, True).wait_recv()
                pass_load(3, 1, j, u).start()
            for j in range(2):
                for side in range(2):
                    pass_load(3, side, j, u).wait()

        for x in range(3):
            for j in range(2):
                for side in range(2):
                    pass_load(x, side, j, u).wait()

        split_queries(u % 2, count)

        def score_block(b, c):
            part[u, :, block_cols(b)] = scores(count, b)
            for k in range(1, n_co):
                part_copy(k, u, b).start()

            @pl.when((u == passes - 1) & (b < LEAD2))
            def _():
                share_diag(tail_first + b)
                tail_load(b, 0).start()

            @pl.when((u == passes - 1) & (b > 0) & (b <= LEAD2))
            def _():
                sib_copy(3, tail_first + b - 1, True).wait_recv()
                tail_load(b - 1, 1).start()

            return c

        lax.fori_loop(0, blocks, score_block, 0)

        @pl.when(u == 1)
        def _():
            for k in range(1, n_co):
                sq_copy(k).wait_recv()

        @pl.when((u > 0) & (u < passes - 1))
        def _():
            finish(u - 1)

        return c

    lax.fori_loop(0, passes, one_pass, 0)

    for i in range(blocks, LEAD2):
        share_diag(tail_first + i)
        tail_load(i, 0).start()
    for i in range(min(blocks, LEAD2) - 1, LEAD2):
        sib_copy(3, tail_first + i, True).wait_recv()
        tail_load(i, 1).start()
    for i in range(LEAD2):
        tail_load(i, 0).wait()
        tail_load(i, 1).wait()
    split_queries(passes % 2, tail_rows)

    def tail_block(b, c):
        @pl.when(b < blocks)
        def _():
            tail_part[:, block_cols(b)] = scores(tail_rows, b)

        ready = b - depth

        @pl.when((co != diag) & (ready >= 0) & (ready < blocks))
        def _():
            @pl.when(depth > 0)
            def _():
                tail_copy(above, ready).wait_recv()
                cols = block_cols(ready)
                tail_part[:, cols] = tail_part[:, cols] + tail_got[above, :, cols]

            tail_copy(above, ready).start()

        return c

    lax.fori_loop(0, blocks + n_co - 2, tail_block, 0)
    finish(passes - 2)
    finish(passes - 1)

    @pl.when(co == diag)
    def _():
        def gather_side(slot):
            for b in range(blocks):
                tail_copy(slot, b).wait_recv()
            tail_part[...] = tail_part[...] + tail_got[slot]

        @pl.when(co > 0)
        def _():
            gather_side(0)

        @pl.when(co < n_co - 1)
        def _():
            gather_side(1)

        moved = settle(tail_part[...])
        for i in range(2):
            at = i * pieces * rows + tail_first * rows
            out_ref[at:at + LEAD2 * rows, :] = moved[i * LEAD2 * rows:(i + 1) * LEAD2 * rows]

    @pl.when(co != diag)
    def _():
        for b in range(blocks):
            tail_copy(above, b).wait_send()

    def drain(p, c):
        for way in range(2):
            own_copy(way, p, False).wait_send()
            relay_copy(way, p, False).wait_send()
        for x in range(4):
            sib_copy(x, p, False).wait_send()
        return c

    lax.fori_loop(0, pieces, drain, 0)

    def drain_parts(u, c):
        for k in range(1, n_co):
            for b in range(blocks):
                part_copy(k, u, b).wait_send()
        return c

    lax.fori_loop(0, passes, drain_parts, 0)
    for k in range(1, n_co):
        sq_copy(k).wait_send()


def plane_shards(n_ex, n_co, train_grads, queries, module_ids, module_scale, example_ids):
    examples, width = train_grads.shape
    pieces = queries.shape[0] // 8
    count = n_ex * 16
    owned = 32
    tail_rows = 2 * LEAD2 * 8
    f32, bf16 = jnp.float32, jnp.bfloat16
    dma = pltpu.SemaphoreType.DMA
    smem = pl.BlockSpec(memory_space=pltpu.SMEM)
    hbm = pl.BlockSpec(memory_space=pl.ANY)
    vmem = pl.BlockSpec(memory_space=pltpu.VMEM)
    scores, _ = pl.pallas_call(
        functools.partial(plane_kernel, n_ex, n_co),
        out_shape=(
            jax.ShapeDtypeStruct((2 * queries.shape[0], examples), f32),
            jax.ShapeDtypeStruct((pieces, n_ex, 8, width), f32),
        ),
        in_specs=[smem, smem, hbm, hbm, vmem],
        out_specs=(vmem, hbm),
        scratch_shapes=[
            pltpu.VMEM((width, examples), bf16),
            pltpu.VMEM((width, examples), bf16),
            pltpu.VMEM((2, 128, width), f32),
            pltpu.VMEM((2 * count, width), bf16),
            pltpu.VMEM((pieces // 2, count, examples), f32),
            pltpu.VMEM((n_co - 1, pieces // 2, owned, examples), f32),
            pltpu.VMEM((tail_rows, examples), f32),
            pltpu.VMEM((2, tail_rows, examples), f32),
            pltpu.VMEM((examples, examples), bf16),
            pltpu.VMEM((8, examples), f32),
            pltpu.VMEM((n_co - 1, 8, examples), f32),
            dma((2, pieces)),
            dma((2, pieces)),
            dma((2, pieces)),
            dma((2, pieces)),
            dma((4, pieces)),
            dma((4, pieces)),
            dma((n_co - 1, pieces // 2, examples // 256)),
            dma((n_co - 1, pieces // 2, examples // 256)),
            dma((examples // 256,)),
            dma((2, examples // 256)),
            dma((n_co - 1,)),
            dma((n_co - 1,)),
            dma((4, 2, 2)),
            dma((2,)),
        ],
        compiler_params=pltpu.CompilerParams(
            collective_id=0, has_side_effects=True, vmem_limit_bytes=67043328
        ),
    )(module_ids, module_scale, queries, train_grads, example_ids[None, :])
    return scores


def solution(mesh):
    n_ex, n_co = mesh.shape["ex"], mesh.shape["co"]
    body = plane_shards if n_ex == 8 and n_ex == 2 * n_co else shards
    return jax.shard_map(
        functools.partial(body, n_ex, n_co),
        mesh=mesh,
        in_specs=(P("ex", "co"), P("ex", "co"), P(), P(), P("ex")),
        out_specs=P("co", "ex"),
        check_vma=False,
    )
```

```python
import functools

import jax
import jax.numpy as jnp
from jax import lax
from jax.experimental import pallas as pl
from jax.experimental.pallas import tpu as pltpu
from jax.sharding import PartitionSpec as P

PROJ = 4096
MESH = pl.DeviceIdType.MESH
PIECES = 8
LEAD = 2
CONTRACT_LAST = (((1,), (1,)), ((), ()))

epsilon = 1e-06


def kernel(n_ex, n_co, pieces, q_ref, g_ref, scale_ref, out_ref, buf,
           ghi, glo, fresh, stage, split, part, got, sq_own, sq_got,
           ring_send, ring_recv, sib_send, sib_recv, part_send, part_recv, sq_send, sq_recv, load_sem):
    chips = n_ex // 2
    half = chips // 2
    ex = lax.axis_index("ex")
    co = lax.axis_index("co")
    core = ex % 2

    def snake(pos):
        upper = pos // half
        return pos * (1 - upper) + upper * (half + chips - 1 - pos)

    pos = snake(ex // 2)

    def device_at(step):
        return snake((pos + step + chips) % chips) * 2 + core

    right = device_at(1)
    left = device_at(-1)
    sibling = ex + 1 - 2 * core
    rows = q_ref.shape[0] // pieces
    width = q_ref.shape[1]
    mid = width // 2
    examples = g_ref.shape[0]
    owned = (n_ex // n_co) * rows

    barrier = pltpu.get_barrier_semaphore()
    for other in (right, left, sibling):
        pl.semaphore_signal(barrier, inc=1, device_id={"ex": other}, device_id_type=MESH)
    for k in range(1, n_co):
        pl.semaphore_signal(barrier, inc=1, device_id={"co": (co + k) % n_co}, device_id_type=MESH)
    pl.semaphore_wait(barrier, 3 + n_co - 1)

    def own_rows(s):
        return q_ref.at[pl.ds(pl.multiple_of(s * rows, rows), rows)]

    def ring_copy(way, d, s, arriving):
        back = d if arriving else d - 1
        origin = device_at(-back if way == 0 else back)
        if d == half and half > 1:
            span = pl.ds(way * mid, mid)
        else:
            span = pl.ds(0, width)
        if d == 1 and not arriving:
            src = own_rows(s)
        else:
            src = buf.at[s, origin, :, span]
        return pltpu.make_async_remote_copy(
            src_ref=src,
            dst_ref=buf.at[s, origin, :, span],
            send_sem=ring_send.at[way, d - 1, s],
            recv_sem=ring_recv.at[way, d - 1, s],
            device_id={"ex": right if way == 0 else left},
            device_id_type=MESH,
        )

    def sibling_copy(off, s, arriving):
        origin = device_at(off)
        if arriving:
            origin = origin + 1 - 2 * core
        src = own_rows(s) if off == 0 and not arriving else buf.at[s, origin]
        return pltpu.make_async_remote_copy(
            src_ref=src,
            dst_ref=buf.at[s, origin],
            send_sem=sib_send.at[off, s],
            recv_sem=sib_recv.at[off, s],
            device_id={"ex": sibling},
            device_id_type=MESH,
        )

    block = 256
    blocks = examples // block

    def part_copy(k, s, b):
        owner = (co + k) % n_co
        cols = pl.ds(pl.multiple_of(b * block, block), block)
        return pltpu.make_async_remote_copy(
            src_ref=part.at[s, pl.ds(pl.multiple_of(owner * owned, owned), owned), cols],
            dst_ref=got.at[k - 1, s, :, cols],
            send_sem=part_send.at[k - 1, s, b],
            recv_sem=part_recv.at[k - 1, s, b],
            device_id={"co": owner},
            device_id_type=MESH,
        )

    def sq_copy(k):
        return pltpu.make_async_remote_copy(
            src_ref=sq_own,
            dst_ref=sq_got.at[k - 1],
            send_sem=sq_send.at[k - 1],
            recv_sem=sq_recv.at[k - 1],
            device_id={"co": (co + k) % n_co},
            device_id_type=MESH,
        )

    def send_own(s):
        ring_copy(0, 1, s, False).start()
        ring_copy(1, 1, s, False).start()
        sibling_copy(0, s, False).start()

    for s in range(min(LEAD, pieces)):
        send_own(s)

    def relay(t):
        for d in range(1, half + 1):
            s = t - (d - 1)

            @pl.when((s >= 0) & (s < pieces))
            def _():
                ring_copy(0, d, s, True).wait_recv()
                if d < half:
                    ring_copy(0, d + 1, s, False).start()
                ring_copy(1, d, s, True).wait_recv()
                if d < half:
                    ring_copy(1, d + 1, s, False).start()
                if d == 1:
                    @pl.when(s + LEAD < pieces)
                    def _():
                        send_own(s + LEAD)
                sibling_copy(chips - d, s, False).start()
                if d < half:
                    sibling_copy(d, s, False).start()

    tile = fresh.shape[1]
    tiles = examples // tile
    strip = min(512, width)

    def g_load(i):
        slot = i % 2
        return pltpu.make_async_copy(
            g_ref.at[pl.ds(pl.multiple_of(i * tile, tile), tile)],
            fresh.at[slot],
            load_sem.at[slot],
        )

    g_load(0).start()

    def split_tile(i, sums):
        @pl.when(i + 1 < tiles)
        def _():
            g_load(i + 1).start()

        @pl.when(i == tiles // 2)
        def _():
            relay(0)

        g_load(i).wait()
        slot = i % 2
        dest = pl.multiple_of(i * tile, tile)

        def split_strip(j, total):
            col = pl.ds(pl.multiple_of(j * strip, strip), strip)
            x = fresh[slot, :, col]
            hi = x.astype(jnp.bfloat16)
            ghi[pl.ds(dest, tile), col] = hi
            glo[pl.ds(dest, tile), col] = (x - hi.astype(jnp.float32)).astype(jnp.bfloat16)
            xx = x * x
            for lane in range(0, strip, 128):
                total = total + xx[:, lane:lane + 128]
            return total

        total = lax.fori_loop(0, width // strip, split_strip, jnp.zeros((tile, 128), jnp.float32))
        row = jnp.sum(total.T, axis=0, keepdims=True)
        sq_own[:, pl.ds(dest, tile)] = jnp.broadcast_to(row, (8, tile))
        return sums

    lax.fori_loop(0, tiles, split_tile, 0)
    for k in range(1, n_co):
        sq_copy(k).start()

    depth = min(8192, width)
    count = n_ex * rows

    def load(off, side, s):
        origin = device_at(off)
        if side:
            origin = origin + 1 - 2 * core
        src = own_rows(s) if off == 0 and not side else buf.at[s, origin]
        return pltpu.make_async_copy(
            src,
            stage.at[pl.ds(pl.multiple_of(origin * rows, rows), rows)],
            load_sem.at[2 + off * 2 + side],
        )

    def compute(s):
        for off in range(chips):
            load(off, 0, s).start()
        for off in range(chips):
            sibling_copy(off, s, True).wait_recv()
            load(off, 1, s).start()
        for off in range(chips):
            load(off, 0, s).wait()
            load(off, 1, s).wait()

        def split_queries(j, c):
            col = pl.ds(pl.multiple_of(j * strip, strip), strip)
            x = stage[:, col] * scale_ref[:, col]
            hi = x.astype(jnp.bfloat16)
            split[pl.ds(0, count), col] = hi
            split[pl.ds(count, count), col] = (x - hi.astype(jnp.float32)).astype(jnp.bfloat16)
            return c

        lax.fori_loop(0, width // strip, split_queries, 0)

        def block_scores(b, c):
            ex_rows = pl.ds(pl.multiple_of(b * block, block), block)

            def deepen(j, acc):
                col = pl.ds(pl.multiple_of(j * depth, depth), depth)
                dot = functools.partial(
                    lax.dot_general, dimension_numbers=CONTRACT_LAST, preferred_element_type=jnp.float32
                )
                both = dot(split[:, col], ghi[ex_rows, col])
                small = both[count:] + dot(split[:count, col], glo[ex_rows, col])
                return acc + (small + both[:count])

            acc = lax.fori_loop(0, width // depth, deepen, jnp.zeros((count, block), jnp.float32))
            part[s, :, ex_rows] = acc
            for k in range(1, n_co):
                part_copy(k, s, b).start()
            return c

        lax.fori_loop(0, blocks, block_scores, 0)

    def step(t, c):
        @pl.when(t > 0)
        def _():
            relay(t)

        s = t - (half - 1)

        @pl.when((s >= 0) & (s < pieces))
        def _():
            compute(s)

        return c

    lax.fori_loop(0, pieces + half - 1, step, 0)

    for k in range(1, n_co):
        sq_copy(k).wait_recv()
    squares = sq_own[...]
    for k in range(1, n_co):
        squares = squares + sq_got[k - 1]
    inverse_norm = lax.rsqrt(squares[0:1] + epsilon)

    def finish(s, c):
        for k in range(1, n_co):
            for b in range(blocks):
                part_copy(k, s, b).wait_recv()
        total = part[s, pl.ds(pl.multiple_of(co * owned, owned), owned)]
        for k in range(1, n_co):
            total = total + got[k - 1, s]
        total = total * inverse_norm
        for i in range(n_ex // n_co):
            at = pl.multiple_of(i * rows * pieces + s * rows, rows)
            out_ref[pl.ds(at, rows), :] = total[i * rows:(i + 1) * rows]
        return c

    lax.fori_loop(0, pieces, finish, 0)

    def drain(s, c):
        for way in range(2):
            for d in range(1, half + 1):
                ring_copy(way, d, s, False).wait_send()
        for off in range(chips):
            sibling_copy(off, s, False).wait_send()
        for k in range(1, n_co):
            for b in range(blocks):
                part_copy(k, s, b).wait_send()
        return c

    lax.fori_loop(0, pieces, drain, 0)
    for k in range(1, n_co):
        sq_copy(k).wait_send()


def shards(n_ex, n_co, train_grads, queries, module_ids, module_scale, example_ids):
    examples, width = train_grads.shape
    position = lax.axis_index("co") * width + lax.iota(jnp.int32, width)
    table_index = lax.iota(jnp.int32, module_scale.shape[0])
    picked = jnp.sum(
        jnp.where(module_ids[:, None] == table_index[None, :], module_scale[None, :], 0.0), axis=1
    )
    window_index = lax.iota(jnp.int32, module_ids.shape[0])
    coord_scale = jnp.sum(
        jnp.where((position // PROJ)[:, None] == window_index[None, :], picked[None, :], 0.0), axis=1
    )

    chips = n_ex // 2
    pieces = min(PIECES, queries.shape[0] // 8)
    rows = queries.shape[0] // pieces
    count = n_ex * rows
    owned = (n_ex // n_co) * rows
    f32, bf16 = jnp.float32, jnp.bfloat16
    dma = pltpu.SemaphoreType.DMA
    normed, _ = pl.pallas_call(
        functools.partial(kernel, n_ex, n_co, pieces),
        out_shape=(
            jax.ShapeDtypeStruct((owned * pieces, examples), f32),
            jax.ShapeDtypeStruct((pieces, n_ex, rows, width), f32),
        ),
        in_specs=[
            pl.BlockSpec(memory_space=pl.ANY),
            pl.BlockSpec(memory_space=pl.ANY),
            pl.BlockSpec(memory_space=pltpu.VMEM),
        ],
        out_specs=(pl.BlockSpec(memory_space=pltpu.VMEM), pl.BlockSpec(memory_space=pl.ANY)),
        scratch_shapes=[
            pltpu.VMEM((examples, width), bf16),
            pltpu.VMEM((examples, width), bf16),
            pltpu.VMEM((2, min(128, examples), width), f32),
            pltpu.VMEM((count, width), f32),
            pltpu.VMEM((2 * count, width), bf16),
            pltpu.VMEM((pieces, count, examples), f32),
            pltpu.VMEM((n_co - 1, pieces, owned, examples), f32),
            pltpu.VMEM((8, examples), f32),
            pltpu.VMEM((n_co - 1, 8, examples), f32),
            dma((2, chips // 2, pieces)),
            dma((2, chips // 2, pieces)),
            dma((chips, pieces)),
            dma((chips, pieces)),
            dma((n_co - 1, pieces, examples // 256)),
            dma((n_co - 1, pieces, examples // 256)),
            dma((n_co - 1,)),
            dma((n_co - 1,)),
            dma((2 + n_ex,)),
        ],
        compiler_params=pltpu.CompilerParams(
            collective_id=0, has_side_effects=True, vmem_limit_bytes=67043328
        ),
    )(queries, train_grads, coord_scale[None, :])

    local_ids = example_ids - lax.axis_index("ex") * examples
    place = (local_ids[:, None] == lax.iota(jnp.int32, examples)[None, :]).astype(f32)
    return lax.dot_general(
        normed, place, (((1,), (0,)), ((), ())), precision=lax.Precision.HIGH, preferred_element_type=f32
    )


AHEAD = 2
UNIT = 16


def plane_kernel(n_ex, n_co, ids_any, table_any, q_ref, g_ref, cols_any, out_ref, buf,
                 ids_ref, table_ref, cols_ref, small_sem, ghi, glo, stage, split, part, got, tail_part, tail_got, place, sq_own, sq_got,
                 own_send, own_recv, rel_send, rel_recv, sib_send, sib_recv,
                 part_send, part_recv, tail_send, tail_recv, sq_send, sq_recv, load_sem, g_sem):
    ex = lax.axis_index("ex")
    co = lax.axis_index("co")
    core = ex % 2
    chip = ex // 2
    cx = chip % 2
    cy = chip // 2
    rows = UNIT
    pieces = q_ref.shape[0] // rows
    width = q_ref.shape[1]
    mid = width // 2
    examples = g_ref.shape[0]
    count = n_ex * rows
    owned = 2 * rows
    early = 4 * rows
    tail_rows = 2 * AHEAD * rows
    tail_first = pieces - AHEAD

    def chip_at(x):
        fx = cx if x % 2 == 0 else 1 - cx
        fy = cy if x < 2 else 1 - cy
        return fy * 2 + fx

    diag = chip_at(3)
    sibling = ex + 1 - 2 * core
    near = [chip_at(1) * 2 + core, chip_at(2) * 2 + core]

    def origin(x, side):
        return chip_at(x) * 2 + (core if side == 0 else 1 - core)

    def band(owner):
        fx = (cx + owner % 2) % 2
        fy = (cy + owner // 2) % 2
        place_of = 2 * fx + 3 * fy - 4 * fx * fy
        return pl.ds(pl.multiple_of(place_of * owned, owned), owned)

    barrier = pltpu.get_barrier_semaphore()
    for other in (near[0], near[1], sibling):
        pl.semaphore_signal(barrier, inc=1, device_id={"ex": other}, device_id_type=MESH)
    for k in range(1, n_co):
        pl.semaphore_signal(barrier, inc=1, device_id={"co": (co + k) % n_co}, device_id_type=MESH)
    pl.semaphore_wait(barrier, 3 + n_co - 1)

    def own_rows(p):
        return q_ref.at[pl.ds(pl.multiple_of(p * rows, rows), rows)]

    def own_copy(way, p, arriving):
        src = chip_at(way + 1) * 2 + core if arriving else ex
        return pltpu.make_async_remote_copy(
            src_ref=own_rows(p),
            dst_ref=buf.at[p, src],
            send_sem=own_send.at[way, p],
            recv_sem=own_recv.at[way, p],
            device_id={"ex": near[way]},
            device_id_type=MESH,
        )

    def relay_copy(way, p, arriving):
        src = origin(3, 0) if arriving else near[1 - way]
        span = pl.ds(way * mid, mid)
        return pltpu.make_async_remote_copy(
            src_ref=buf.at[p, src, :, span],
            dst_ref=buf.at[p, src, :, span],
            send_sem=rel_send.at[way, p],
            recv_sem=rel_recv.at[way, p],
            device_id={"ex": near[way]},
            device_id_type=MESH,
        )

    def sib_copy(x, p, arriving):
        src = origin(x, 1 if arriving else 0)
        return pltpu.make_async_remote_copy(
            src_ref=own_rows(p) if x == 0 else buf.at[p, src],
            dst_ref=buf.at[p, src],
            send_sem=sib_send.at[x, p],
            recv_sem=sib_recv.at[x, p],
            device_id={"ex": sibling},
            device_id_type=MESH,
        )

    block = 256
    blocks = examples // block

    def block_cols(b):
        return pl.ds(pl.multiple_of(b * block, block), block)

    def part_copy(k, u, b):
        owner = (co + k) % n_co
        return pltpu.make_async_remote_copy(
            src_ref=part.at[u, band(owner), block_cols(b)],
            dst_ref=got.at[k - 1, u, :, block_cols(b)],
            send_sem=part_send.at[k - 1, u, b],
            recv_sem=part_recv.at[k - 1, u, b],
            device_id={"co": owner},
            device_id_type=MESH,
        )

    above = (co > diag).astype(jnp.int32)
    depth = co + above * (n_co - 1 - 2 * co)

    def grain(g):
        return pl.ds(g * rows, rows)

    grains = tail_rows // rows

    def tail_copy(slot, b, g):
        return pltpu.make_async_remote_copy(
            src_ref=tail_part.at[grain(g), block_cols(b)],
            dst_ref=tail_got.at[slot, grain(g), block_cols(b)],
            send_sem=tail_send.at[b, g],
            recv_sem=tail_recv.at[slot, b, g],
            device_id={"co": (co + 1 - 2 * slot + n_co) % n_co},
            device_id_type=MESH,
        )

    def sq_copy(k):
        return pltpu.make_async_remote_copy(
            src_ref=sq_own,
            dst_ref=sq_got.at[k - 1],
            send_sem=sq_send.at[k - 1],
            recv_sem=sq_recv.at[k - 1],
            device_id={"co": (co + k) % n_co},
            device_id_type=MESH,
        )

    def send_own(p):
        own_copy(0, p, False).start()
        own_copy(1, p, False).start()
        sib_copy(0, p, False).start()

    for p in range(AHEAD):
        send_own(p)

    def forward(p):
        own_copy(1, p, True).wait_recv()
        relay_copy(0, p, False).start()
        own_copy(0, p, True).wait_recv()
        relay_copy(1, p, False).start()

        @pl.when(p + AHEAD < pieces)
        def _():
            send_own(p + AHEAD)

        sib_copy(1, p, False).start()
        sib_copy(2, p, False).start()

    def share_diag(p):
        relay_copy(0, p, True).wait_recv()
        relay_copy(1, p, True).wait_recv()
        sib_copy(3, p, False).start()

    tile = stage.shape[1]
    tiles = examples // tile
    strip = min(512, width)

    def g_load(i):
        return pltpu.make_async_copy(
            g_ref.at[pl.ds(pl.multiple_of(i * tile, tile), tile)], stage.at[i % 2], g_sem.at[i % 2]
        )

    g_load(0).start()
    smalls = [
        pltpu.make_async_copy(src, dst, small_sem.at[i])
        for i, (src, dst) in enumerate([(ids_any, ids_ref), (table_any, table_ref), (cols_any, cols_ref)])
    ]
    for copy in smalls:
        copy.start()
    for copy in smalls:
        copy.wait()

    local = cols_ref[...] - ex * examples
    for i in range(examples // 128):
        spot = lax.broadcasted_iota(jnp.int32, (128, examples), 0) + i * 128
        hot = (spot == local).astype(jnp.float32).astype(jnp.bfloat16)
        place[:, i * 128:(i + 1) * 128] = hot.T

    def split_tile(i, c):
        @pl.when(i + 1 < tiles)
        def _():
            g_load(i + 1).start()

        @pl.when(i == tiles - 2)
        def _():
            forward(0)

        g_load(i).wait()
        slot = i % 2
        dest = pl.ds(pl.multiple_of(i * tile, tile), tile)

        def split_strip(j, total):
            col = pl.ds(pl.multiple_of(j * strip, strip), strip)
            x = stage[slot, :, col]
            hi = x.astype(jnp.bfloat16)
            ghi[col, dest] = hi.T
            glo[col, dest] = (x - hi.astype(jnp.float32)).astype(jnp.bfloat16).T
            xx = x * x
            for lane in range(0, strip, 128):
                total = total + xx[:, lane:lane + 128]
            return total

        total = lax.fori_loop(0, width // strip, split_strip, jnp.zeros((tile, 128), jnp.float32))
        row = jnp.sum(total.T, axis=0, keepdims=True)
        sq_own[:, dest] = jnp.broadcast_to(row, (8, tile))
        return c

    lax.fori_loop(0, tiles, split_tile, 0)
    for k in range(1, n_co):
        sq_copy(k).start()

    def load(x, side, p, slot, row, sem):
        src = own_rows(p) if x == 0 and side == 0 else buf.at[p, origin(x, side)]
        return pltpu.make_async_copy(src, stage.at[slot, pl.ds(pl.multiple_of(row, rows), rows)], sem)

    def pass_load(x, side, u):
        p = u - (AHEAD if x == 3 else 0)
        at = (0, 2, 3, 1)[x] * owned + (core if side == 0 else 1 - core) * rows
        return load(x, side, p, u % 2, at, load_sem.at[x, side])

    def tail_load(i, side):
        at = (core if side == 0 else 1 - core) * (AHEAD * rows) + i * rows
        return load(3, side, tail_first + i, pieces % 2, at, load_sem.at[i, side])

    def split_queries(slot, first, size, m):
        def body(j, c):
            col = pl.ds(pl.multiple_of(j * strip, strip), strip)
            scale = table_ref[ids_ref[(co * width + j * strip) // PROJ]]
            x = stage[slot, first:first + size, col] * scale
            hi = x.astype(jnp.bfloat16)
            split[first:first + size, col] = hi
            split[m + first:m + first + size, col] = (x - hi.astype(jnp.float32)).astype(jnp.bfloat16)
            return c

        lax.fori_loop(0, width // strip, body, 0)

    def scores(m, b):
        cols = block_cols(b)
        both = jnp.dot(split[:2 * m, :], ghi[:, cols], preferred_element_type=jnp.float32)
        small = both[m:] + jnp.dot(split[:m, :], glo[:, cols], preferred_element_type=jnp.float32)
        return small + both[:m]

    def settle(total):
        squares = sq_own[...]
        for k in range(1, n_co):
            squares = squares + sq_got[k - 1]
        total = total * lax.rsqrt(squares[0:1] + epsilon)
        m = total.shape[0]
        hi = total.astype(jnp.bfloat16)
        rest = total - hi.astype(jnp.float32)
        half = rest.astype(jnp.bfloat16)
        last = (rest - half.astype(jnp.float32)).astype(jnp.bfloat16)
        three = jnp.concatenate([hi, half, last], axis=0)
        moved = jnp.dot(three, place[...], preferred_element_type=jnp.float32)
        return moved[:m] + (moved[m:2 * m] + moved[2 * m:])

    def finish(u):
        for k in range(1, n_co):
            for b in range(blocks):
                part_copy(k, u, b).wait_recv()
        lag = (co == diag).astype(jnp.int32) * AHEAD
        first = u - lag

        @pl.when(first >= 0)
        def _():
            total = part[u, band(co)]
            for k in range(1, n_co):
                total = total + got[k - 1, u]
            moved = settle(total)
            for i in range(2):
                at = pl.multiple_of(i * pieces * rows + first * rows, rows)
                out_ref[pl.ds(at, rows), :] = moved[i * rows:(i + 1) * rows]

    def early_own(u):
        pass_load(0, 0, u).start()

        @pl.when(u >= AHEAD)
        def _():
            share_diag(u - AHEAD)
            pass_load(3, 0, u).start()

    def early_sibling(u):
        sib_copy(0, u, True).wait_recv()
        pass_load(0, 1, u).start()

        @pl.when(u >= AHEAD)
        def _():
            sib_copy(3, u - AHEAD, True).wait_recv()
            pass_load(3, 1, u).start()

    early_own(0)
    early_sibling(0)

    def one_pass(u, c):
        for side in range(2):
            pass_load(0, side, u).wait()

        @pl.when(u >= AHEAD)
        def _():
            for side in range(2):
                pass_load(3, side, u).wait()

        split_queries(u % 2, 0, early, count)

        @pl.when(u > 1)
        def _():
            forward(u)

        for x in (1, 2):
            pass_load(x, 0, u).start()
        for x in (1, 2):
            sib_copy(x, u, True).wait_recv()
            pass_load(x, 1, u).start()
        for x in (1, 2):
            for side in range(2):
                pass_load(x, side, u).wait()
        split_queries(u % 2, early, count - early, count)

        def score_block(b, c):
            part[u, :, block_cols(b)] = scores(count, b)
            for k in range(1, n_co):
                part_copy(k, u, b).start()

            @pl.when((u == 0) & (b == 0))
            def _():
                forward(1)

            @pl.when((u < pieces - 1) & (b == 1))
            def _():
                early_own(u + 1)

            @pl.when((u < pieces - 1) & (b == 2))
            def _():
                early_sibling(u + 1)

            @pl.when((u == pieces - 1) & (b == 1))
            def _():
                share_diag(tail_first)
                tail_load(0, 0).start()

            @pl.when((u == pieces - 1) & (b == 2))
            def _():
                sib_copy(3, tail_first, True).wait_recv()
                tail_load(0, 1).start()
                share_diag(tail_first + 1)
                tail_load(1, 0).start()

            return c

        lax.fori_loop(0, blocks, score_block, 0)

        @pl.when(u == 1)
        def _():
            for k in range(1, n_co):
                sq_copy(k).wait_recv()

        @pl.when((u > 0) & (u < pieces - 1))
        def _():
            finish(u - 1)

        return c

    lax.fori_loop(0, pieces, one_pass, 0)

    sib_copy(3, tail_first + 1, True).wait_recv()
    tail_load(1, 1).start()
    for i in range(AHEAD):
        tail_load(i, 0).wait()
        tail_load(i, 1).wait()
    split_queries(pieces % 2, 0, tail_rows, tail_rows)

    def tail_block(b, c):
        @pl.when(b < blocks)
        def _():
            tail_part[:, block_cols(b)] = scores(tail_rows, b)

        ready = b - depth

        @pl.when((co != diag) & (ready >= 0) & (ready < blocks))
        def _():
            cols = block_cols(ready)
            for g in range(grains):
                @pl.when(depth > 0)
                def _():
                    tail_copy(above, ready, g).wait_recv()
                    tail_part[grain(g), cols] = tail_part[grain(g), cols] + tail_got[above, grain(g), cols]

                tail_copy(above, ready, g).start()

        return c

    lax.fori_loop(0, blocks + n_co - 2, tail_block, 0)
    finish(pieces - 2)
    finish(pieces - 1)

    @pl.when(co == diag)
    def _():
        def gather_side(slot):
            for b in range(blocks):
                for g in range(grains):
                    tail_copy(slot, b, g).wait_recv()
            tail_part[...] = tail_part[...] + tail_got[slot]

        @pl.when(co > 0)
        def _():
            gather_side(0)

        @pl.when(co < n_co - 1)
        def _():
            gather_side(1)

        moved = settle(tail_part[...])
        for i in range(2):
            at = i * pieces * rows + tail_first * rows
            out_ref[at:at + AHEAD * rows, :] = moved[i * AHEAD * rows:(i + 1) * AHEAD * rows]

    @pl.when(co != diag)
    def _():
        for b in range(blocks):
            for g in range(grains):
                tail_copy(above, b, g).wait_send()

    def drain(p, c):
        for way in range(2):
            own_copy(way, p, False).wait_send()
            relay_copy(way, p, False).wait_send()
        for x in range(4):
            sib_copy(x, p, False).wait_send()
        return c

    lax.fori_loop(0, pieces, drain, 0)

    def drain_parts(u, c):
        for k in range(1, n_co):
            for b in range(blocks):
                part_copy(k, u, b).wait_send()
        return c

    lax.fori_loop(0, pieces, drain_parts, 0)
    for k in range(1, n_co):
        sq_copy(k).wait_send()


def plane_shards(n_ex, n_co, train_grads, queries, module_ids, module_scale, example_ids):
    examples, width = train_grads.shape
    pieces = queries.shape[0] // UNIT
    count = n_ex * UNIT
    owned = 2 * UNIT
    tail_rows = 2 * AHEAD * UNIT
    f32, bf16 = jnp.float32, jnp.bfloat16
    dma = pltpu.SemaphoreType.DMA
    hbm = pl.BlockSpec(memory_space=pl.ANY)
    vmem = pl.BlockSpec(memory_space=pltpu.VMEM)
    scores, _ = pl.pallas_call(
        functools.partial(plane_kernel, n_ex, n_co),
        out_shape=(
            jax.ShapeDtypeStruct((2 * queries.shape[0], examples), f32),
            jax.ShapeDtypeStruct((pieces, n_ex, UNIT, width), f32),
        ),
        in_specs=[hbm, hbm, hbm, hbm, hbm],
        out_specs=(vmem, hbm),
        scratch_shapes=[
            pltpu.SMEM(module_ids.shape, jnp.int32),
            pltpu.SMEM(module_scale.shape, f32),
            pltpu.VMEM((1, examples), jnp.int32),
            dma((3,)),
            pltpu.VMEM((width, examples), bf16),
            pltpu.VMEM((width, examples), bf16),
            pltpu.VMEM((2, 128, width), f32),
            pltpu.VMEM((2 * count, width), bf16),
            pltpu.VMEM((pieces, count, examples), f32),
            pltpu.VMEM((n_co - 1, pieces, owned, examples), f32),
            pltpu.VMEM((tail_rows, examples), f32),
            pltpu.VMEM((2, tail_rows, examples), f32),
            pltpu.VMEM((examples, examples), bf16),
            pltpu.VMEM((8, examples), f32),
            pltpu.VMEM((n_co - 1, 8, examples), f32),
            dma((2, pieces)),
            dma((2, pieces)),
            dma((2, pieces)),
            dma((2, pieces)),
            dma((4, pieces)),
            dma((4, pieces)),
            dma((n_co - 1, pieces, examples // 256)),
            dma((n_co - 1, pieces, examples // 256)),
            dma((examples // 256, 2 * AHEAD)),
            dma((2, examples // 256, 2 * AHEAD)),
            dma((n_co - 1,)),
            dma((n_co - 1,)),
            dma((4, 2)),
            dma((2,)),
        ],
        compiler_params=pltpu.CompilerParams(
            collective_id=0, has_side_effects=True, vmem_limit_bytes=67043328
        ),
    )(module_ids, module_scale, queries, train_grads, example_ids[None, :])
    return scores


def solution(mesh):
    n_ex, n_co = mesh.shape["ex"], mesh.shape["co"]
    body = plane_shards if n_ex == 8 and n_ex == 2 * n_co else shards
    return jax.shard_map(
        functools.partial(body, n_ex, n_co),
        mesh=mesh,
        in_specs=(P("ex", "co"), P("ex", "co"), P(), P(), P("ex")),
        out_specs=P("co", "ex"),
        check_vma=False,
    )
```

```python
import functools

import jax
import jax.numpy as jnp
from jax import lax
from jax.experimental import pallas as pl
from jax.experimental.pallas import tpu as pltpu
from jax.sharding import PartitionSpec as P

PROJ = 4096
MESH = pl.DeviceIdType.MESH
PIECES = 8
LEAD = 2
CONTRACT_LAST = (((1,), (1,)), ((), ()))

epsilon = 1e-06


def kernel(n_ex, n_co, pieces, q_ref, g_ref, scale_ref, out_ref, buf,
           ghi, glo, fresh, stage, split, part, got, sq_own, sq_got,
           ring_send, ring_recv, sib_send, sib_recv, part_send, part_recv, sq_send, sq_recv, load_sem):
    chips = n_ex // 2
    half = chips // 2
    ex = lax.axis_index("ex")
    co = lax.axis_index("co")
    core = ex % 2

    def snake(pos):
        upper = pos // half
        return pos * (1 - upper) + upper * (half + chips - 1 - pos)

    pos = snake(ex // 2)

    def device_at(step):
        return snake((pos + step + chips) % chips) * 2 + core

    right = device_at(1)
    left = device_at(-1)
    sibling = ex + 1 - 2 * core
    rows = q_ref.shape[0] // pieces
    width = q_ref.shape[1]
    mid = width // 2
    examples = g_ref.shape[0]
    owned = (n_ex // n_co) * rows

    barrier = pltpu.get_barrier_semaphore()
    for other in (right, left, sibling):
        pl.semaphore_signal(barrier, inc=1, device_id={"ex": other}, device_id_type=MESH)
    for k in range(1, n_co):
        pl.semaphore_signal(barrier, inc=1, device_id={"co": (co + k) % n_co}, device_id_type=MESH)
    pl.semaphore_wait(barrier, 3 + n_co - 1)

    def own_rows(s):
        return q_ref.at[pl.ds(pl.multiple_of(s * rows, rows), rows)]

    def ring_copy(way, d, s, arriving):
        back = d if arriving else d - 1
        origin = device_at(-back if way == 0 else back)
        if d == half and half > 1:
            span = pl.ds(way * mid, mid)
        else:
            span = pl.ds(0, width)
        if d == 1 and not arriving:
            src = own_rows(s)
        else:
            src = buf.at[s, origin, :, span]
        return pltpu.make_async_remote_copy(
            src_ref=src,
            dst_ref=buf.at[s, origin, :, span],
            send_sem=ring_send.at[way, d - 1, s],
            recv_sem=ring_recv.at[way, d - 1, s],
            device_id={"ex": right if way == 0 else left},
            device_id_type=MESH,
        )

    def sibling_copy(off, s, arriving):
        origin = device_at(off)
        if arriving:
            origin = origin + 1 - 2 * core
        src = own_rows(s) if off == 0 and not arriving else buf.at[s, origin]
        return pltpu.make_async_remote_copy(
            src_ref=src,
            dst_ref=buf.at[s, origin],
            send_sem=sib_send.at[off, s],
            recv_sem=sib_recv.at[off, s],
            device_id={"ex": sibling},
            device_id_type=MESH,
        )

    block = 256
    blocks = examples // block

    def part_copy(k, s, b):
        owner = (co + k) % n_co
        cols = pl.ds(pl.multiple_of(b * block, block), block)
        return pltpu.make_async_remote_copy(
            src_ref=part.at[s, pl.ds(pl.multiple_of(owner * owned, owned), owned), cols],
            dst_ref=got.at[k - 1, s, :, cols],
            send_sem=part_send.at[k - 1, s, b],
            recv_sem=part_recv.at[k - 1, s, b],
            device_id={"co": owner},
            device_id_type=MESH,
        )

    def sq_copy(k):
        return pltpu.make_async_remote_copy(
            src_ref=sq_own,
            dst_ref=sq_got.at[k - 1],
            send_sem=sq_send.at[k - 1],
            recv_sem=sq_recv.at[k - 1],
            device_id={"co": (co + k) % n_co},
            device_id_type=MESH,
        )

    def send_own(s):
        ring_copy(0, 1, s, False).start()
        ring_copy(1, 1, s, False).start()
        sibling_copy(0, s, False).start()

    for s in range(min(LEAD, pieces)):
        send_own(s)

    def relay(t):
        for d in range(1, half + 1):
            s = t - (d - 1)

            @pl.when((s >= 0) & (s < pieces))
            def _():
                ring_copy(0, d, s, True).wait_recv()
                if d < half:
                    ring_copy(0, d + 1, s, False).start()
                ring_copy(1, d, s, True).wait_recv()
                if d < half:
                    ring_copy(1, d + 1, s, False).start()
                if d == 1:
                    @pl.when(s + LEAD < pieces)
                    def _():
                        send_own(s + LEAD)
                sibling_copy(chips - d, s, False).start()
                if d < half:
                    sibling_copy(d, s, False).start()

    tile = fresh.shape[1]
    tiles = examples // tile
    strip = min(512, width)

    def g_load(i):
        slot = i % 2
        return pltpu.make_async_copy(
            g_ref.at[pl.ds(pl.multiple_of(i * tile, tile), tile)],
            fresh.at[slot],
            load_sem.at[slot],
        )

    g_load(0).start()

    def split_tile(i, sums):
        @pl.when(i + 1 < tiles)
        def _():
            g_load(i + 1).start()

        @pl.when(i == tiles // 2)
        def _():
            relay(0)

        g_load(i).wait()
        slot = i % 2
        dest = pl.multiple_of(i * tile, tile)

        def split_strip(j, total):
            col = pl.ds(pl.multiple_of(j * strip, strip), strip)
            x = fresh[slot, :, col]
            hi = x.astype(jnp.bfloat16)
            ghi[pl.ds(dest, tile), col] = hi
            glo[pl.ds(dest, tile), col] = (x - hi.astype(jnp.float32)).astype(jnp.bfloat16)
            xx = x * x
            for lane in range(0, strip, 128):
                total = total + xx[:, lane:lane + 128]
            return total

        total = lax.fori_loop(0, width // strip, split_strip, jnp.zeros((tile, 128), jnp.float32))
        row = jnp.sum(total.T, axis=0, keepdims=True)
        sq_own[:, pl.ds(dest, tile)] = jnp.broadcast_to(row, (8, tile))
        return sums

    lax.fori_loop(0, tiles, split_tile, 0)
    for k in range(1, n_co):
        sq_copy(k).start()

    depth = min(8192, width)
    count = n_ex * rows

    def load(off, side, s):
        origin = device_at(off)
        if side:
            origin = origin + 1 - 2 * core
        src = own_rows(s) if off == 0 and not side else buf.at[s, origin]
        return pltpu.make_async_copy(
            src,
            stage.at[pl.ds(pl.multiple_of(origin * rows, rows), rows)],
            load_sem.at[2 + off * 2 + side],
        )

    def compute(s):
        for off in range(chips):
            load(off, 0, s).start()
        for off in range(chips):
            sibling_copy(off, s, True).wait_recv()
            load(off, 1, s).start()
        for off in range(chips):
            load(off, 0, s).wait()
            load(off, 1, s).wait()

        def split_queries(j, c):
            col = pl.ds(pl.multiple_of(j * strip, strip), strip)
            x = stage[:, col] * scale_ref[:, col]
            hi = x.astype(jnp.bfloat16)
            split[pl.ds(0, count), col] = hi
            split[pl.ds(count, count), col] = (x - hi.astype(jnp.float32)).astype(jnp.bfloat16)
            return c

        lax.fori_loop(0, width // strip, split_queries, 0)

        def block_scores(b, c):
            ex_rows = pl.ds(pl.multiple_of(b * block, block), block)

            def deepen(j, acc):
                col = pl.ds(pl.multiple_of(j * depth, depth), depth)
                dot = functools.partial(
                    lax.dot_general, dimension_numbers=CONTRACT_LAST, preferred_element_type=jnp.float32
                )
                both = dot(split[:, col], ghi[ex_rows, col])
                small = both[count:] + dot(split[:count, col], glo[ex_rows, col])
                return acc + (small + both[:count])

            acc = lax.fori_loop(0, width // depth, deepen, jnp.zeros((count, block), jnp.float32))
            part[s, :, ex_rows] = acc
            for k in range(1, n_co):
                part_copy(k, s, b).start()
            return c

        lax.fori_loop(0, blocks, block_scores, 0)

    def step(t, c):
        @pl.when(t > 0)
        def _():
            relay(t)

        s = t - (half - 1)

        @pl.when((s >= 0) & (s < pieces))
        def _():
            compute(s)

        return c

    lax.fori_loop(0, pieces + half - 1, step, 0)

    for k in range(1, n_co):
        sq_copy(k).wait_recv()
    squares = sq_own[...]
    for k in range(1, n_co):
        squares = squares + sq_got[k - 1]
    inverse_norm = lax.rsqrt(squares[0:1] + epsilon)

    def finish(s, c):
        for k in range(1, n_co):
            for b in range(blocks):
                part_copy(k, s, b).wait_recv()
        total = part[s, pl.ds(pl.multiple_of(co * owned, owned), owned)]
        for k in range(1, n_co):
            total = total + got[k - 1, s]
        total = total * inverse_norm
        for i in range(n_ex // n_co):
            at = pl.multiple_of(i * rows * pieces + s * rows, rows)
            out_ref[pl.ds(at, rows), :] = total[i * rows:(i + 1) * rows]
        return c

    lax.fori_loop(0, pieces, finish, 0)

    def drain(s, c):
        for way in range(2):
            for d in range(1, half + 1):
                ring_copy(way, d, s, False).wait_send()
        for off in range(chips):
            sibling_copy(off, s, False).wait_send()
        for k in range(1, n_co):
            for b in range(blocks):
                part_copy(k, s, b).wait_send()
        return c

    lax.fori_loop(0, pieces, drain, 0)
    for k in range(1, n_co):
        sq_copy(k).wait_send()


def shards(n_ex, n_co, train_grads, queries, module_ids, module_scale, example_ids):
    examples, width = train_grads.shape
    position = lax.axis_index("co") * width + lax.iota(jnp.int32, width)
    table_index = lax.iota(jnp.int32, module_scale.shape[0])
    picked = jnp.sum(
        jnp.where(module_ids[:, None] == table_index[None, :], module_scale[None, :], 0.0), axis=1
    )
    window_index = lax.iota(jnp.int32, module_ids.shape[0])
    coord_scale = jnp.sum(
        jnp.where((position // PROJ)[:, None] == window_index[None, :], picked[None, :], 0.0), axis=1
    )

    chips = n_ex // 2
    pieces = min(PIECES, queries.shape[0] // 8)
    rows = queries.shape[0] // pieces
    count = n_ex * rows
    owned = (n_ex // n_co) * rows
    f32, bf16 = jnp.float32, jnp.bfloat16
    dma = pltpu.SemaphoreType.DMA
    normed, _ = pl.pallas_call(
        functools.partial(kernel, n_ex, n_co, pieces),
        out_shape=(
            jax.ShapeDtypeStruct((owned * pieces, examples), f32),
            jax.ShapeDtypeStruct((pieces, n_ex, rows, width), f32),
        ),
        in_specs=[
            pl.BlockSpec(memory_space=pl.ANY),
            pl.BlockSpec(memory_space=pl.ANY),
            pl.BlockSpec(memory_space=pltpu.VMEM),
        ],
        out_specs=(pl.BlockSpec(memory_space=pltpu.VMEM), pl.BlockSpec(memory_space=pl.ANY)),
        scratch_shapes=[
            pltpu.VMEM((examples, width), bf16),
            pltpu.VMEM((examples, width), bf16),
            pltpu.VMEM((2, min(128, examples), width), f32),
            pltpu.VMEM((count, width), f32),
            pltpu.VMEM((2 * count, width), bf16),
            pltpu.VMEM((pieces, count, examples), f32),
            pltpu.VMEM((n_co - 1, pieces, owned, examples), f32),
            pltpu.VMEM((8, examples), f32),
            pltpu.VMEM((n_co - 1, 8, examples), f32),
            dma((2, chips // 2, pieces)),
            dma((2, chips // 2, pieces)),
            dma((chips, pieces)),
            dma((chips, pieces)),
            dma((n_co - 1, pieces, examples // 256)),
            dma((n_co - 1, pieces, examples // 256)),
            dma((n_co - 1,)),
            dma((n_co - 1,)),
            dma((2 + n_ex,)),
        ],
        compiler_params=pltpu.CompilerParams(
            collective_id=0, has_side_effects=True, vmem_limit_bytes=67043328
        ),
    )(queries, train_grads, coord_scale[None, :])

    local_ids = example_ids - lax.axis_index("ex") * examples
    place = (local_ids[:, None] == lax.iota(jnp.int32, examples)[None, :]).astype(f32)
    return lax.dot_general(
        normed, place, (((1,), (0,)), ((), ())), precision=lax.Precision.HIGH, preferred_element_type=f32
    )


AHEAD = 2
UNIT = 16


def plane_kernel(n_ex, n_co, ids_any, table_any, q_ref, g_ref, cols_any, final_ref, buf,
                 ids_ref, table_ref, cols_ref, small_sem, out_ref, out_sem, ghi, glo, stage, split, tail_split, part, got, tail_part, tail_got, place, sq_own, sq_got,
                 own_send, own_recv, rel_send, rel_recv, sib_send, sib_recv,
                 part_send, part_recv, tail_send, tail_recv, sq_send, sq_recv, load_sem, g_sem):
    ex = lax.axis_index("ex")
    co = lax.axis_index("co")
    core = ex % 2
    chip = ex // 2
    cx = chip % 2
    cy = chip // 2
    rows = UNIT
    pieces = q_ref.shape[0] // rows
    width = q_ref.shape[1]
    mid = width // 2
    examples = g_ref.shape[0]
    count = n_ex * rows
    owned = 2 * rows
    early = 4 * rows
    tail_rows = 2 * AHEAD * rows
    tail_first = pieces - AHEAD

    def chip_at(x):
        fx = cx if x % 2 == 0 else 1 - cx
        fy = cy if x < 2 else 1 - cy
        return fy * 2 + fx

    diag = chip_at(3)
    sibling = ex + 1 - 2 * core
    near = [chip_at(1) * 2 + core, chip_at(2) * 2 + core]

    def origin(x, side):
        return chip_at(x) * 2 + (core if side == 0 else 1 - core)

    def band(owner):
        fx = (cx + owner % 2) % 2
        fy = (cy + owner // 2) % 2
        place_of = 2 * fx + 3 * fy - 4 * fx * fy
        return pl.ds(pl.multiple_of(place_of * owned, owned), owned)

    barrier = pltpu.get_barrier_semaphore()
    for other in (near[0], near[1], sibling):
        pl.semaphore_signal(barrier, inc=1, device_id={"ex": other}, device_id_type=MESH)
    for k in range(1, n_co):
        pl.semaphore_signal(barrier, inc=1, device_id={"co": (co + k) % n_co}, device_id_type=MESH)
    pl.semaphore_wait(barrier, 3 + n_co - 1)

    def own_rows(p):
        return q_ref.at[pl.ds(pl.multiple_of(p * rows, rows), rows)]

    def own_copy(way, p, arriving):
        src = chip_at(way + 1) * 2 + core if arriving else ex
        return pltpu.make_async_remote_copy(
            src_ref=own_rows(p),
            dst_ref=buf.at[p, src],
            send_sem=own_send.at[way, p],
            recv_sem=own_recv.at[way, p],
            device_id={"ex": near[way]},
            device_id_type=MESH,
        )

    def relay_copy(way, p, arriving):
        src = origin(3, 0) if arriving else near[1 - way]
        span = pl.ds(way * mid, mid)
        return pltpu.make_async_remote_copy(
            src_ref=buf.at[p, src, :, span],
            dst_ref=buf.at[p, src, :, span],
            send_sem=rel_send.at[way, p],
            recv_sem=rel_recv.at[way, p],
            device_id={"ex": near[way]},
            device_id_type=MESH,
        )

    def sib_copy(x, p, arriving):
        src = origin(x, 1 if arriving else 0)
        return pltpu.make_async_remote_copy(
            src_ref=own_rows(p) if x == 0 else buf.at[p, src],
            dst_ref=buf.at[p, src],
            send_sem=sib_send.at[x, p],
            recv_sem=sib_recv.at[x, p],
            device_id={"ex": sibling},
            device_id_type=MESH,
        )

    block = 256
    blocks = examples // block

    def block_cols(b):
        return pl.ds(pl.multiple_of(b * block, block), block)

    def part_copy(k, u, b):
        owner = (co + k) % n_co
        return pltpu.make_async_remote_copy(
            src_ref=part.at[u, band(owner), block_cols(b)],
            dst_ref=got.at[k - 1, u, :, block_cols(b)],
            send_sem=part_send.at[k - 1, u, b],
            recv_sem=part_recv.at[k - 1, u, b],
            device_id={"co": owner},
            device_id_type=MESH,
        )

    above = (co > diag).astype(jnp.int32)
    depth = co + above * (n_co - 1 - 2 * co)

    def grain(g):
        return pl.ds(g * rows, rows)

    grains = tail_rows // rows

    def tail_copy(slot, b, g):
        return pltpu.make_async_remote_copy(
            src_ref=tail_part.at[grain(g), block_cols(b)],
            dst_ref=tail_got.at[slot, grain(g), block_cols(b)],
            send_sem=tail_send.at[b, g],
            recv_sem=tail_recv.at[slot, b, g],
            device_id={"co": (co + 1 - 2 * slot + n_co) % n_co},
            device_id_type=MESH,
        )

    def sq_copy(k):
        return pltpu.make_async_remote_copy(
            src_ref=sq_own,
            dst_ref=sq_got.at[k - 1],
            send_sem=sq_send.at[k - 1],
            recv_sem=sq_recv.at[k - 1],
            device_id={"co": (co + k) % n_co},
            device_id_type=MESH,
        )

    def send_own(p):
        own_copy(0, p, False).start()
        own_copy(1, p, False).start()
        sib_copy(0, p, False).start()

    for p in range(AHEAD):
        send_own(p)

    def forward(p):
        own_copy(1, p, True).wait_recv()
        relay_copy(0, p, False).start()
        own_copy(0, p, True).wait_recv()
        relay_copy(1, p, False).start()
        sib_copy(2, p, False).start()
        sib_copy(1, p, False).start()

        @pl.when(p + AHEAD < pieces)
        def _():
            send_own(p + AHEAD)

    def share_diag(p):
        relay_copy(0, p, True).wait_recv()
        relay_copy(1, p, True).wait_recv()
        sib_copy(3, p, False).start()

    tile = stage.shape[1]
    tiles = examples // tile
    strip = min(512, width)

    def g_load(i):
        return pltpu.make_async_copy(
            g_ref.at[pl.ds(pl.multiple_of(i * tile, tile), tile)], stage.at[i % 2], g_sem.at[i % 2]
        )

    g_load(0).start()
    smalls = [
        pltpu.make_async_copy(src, dst, small_sem.at[i])
        for i, (src, dst) in enumerate([(ids_any, ids_ref), (table_any, table_ref), (cols_any, cols_ref)])
    ]
    for copy in smalls:
        copy.start()
    for copy in smalls:
        copy.wait()

    local = cols_ref[...] - ex * examples
    for i in range(examples // 128):
        spot = lax.broadcasted_iota(jnp.int32, (128, examples), 0) + i * 128
        hot = (spot == local).astype(jnp.float32).astype(jnp.bfloat16)
        place[:, i * 128:(i + 1) * 128] = hot.T

    def split_tile(i, c):
        @pl.when(i + 1 < tiles)
        def _():
            g_load(i + 1).start()

        @pl.when(i == tiles - 2)
        def _():
            forward(0)

        g_load(i).wait()
        slot = i % 2
        dest = pl.ds(pl.multiple_of(i * tile, tile), tile)

        def split_strip(j, total):
            col = pl.ds(pl.multiple_of(j * strip, strip), strip)
            x = stage[slot, :, col]
            hi = x.astype(jnp.bfloat16)
            ghi[col, dest] = hi.T
            glo[col, dest] = (x - hi.astype(jnp.float32)).astype(jnp.bfloat16).T
            xx = x * x
            for lane in range(0, strip, 128):
                total = total + xx[:, lane:lane + 128]
            return total

        total = lax.fori_loop(0, width // strip, split_strip, jnp.zeros((tile, 128), jnp.float32))
        row = jnp.sum(total.T, axis=0, keepdims=True)
        sq_own[:, dest] = jnp.broadcast_to(row, (8, tile))
        return c

    lax.fori_loop(0, tiles, split_tile, 0)
    for k in range(1, n_co):
        sq_copy(k).start()

    def load(x, side, p, slot, row, sem):
        src = own_rows(p) if x == 0 and side == 0 else buf.at[p, origin(x, side)]
        return pltpu.make_async_copy(src, stage.at[slot, pl.ds(pl.multiple_of(row, rows), rows)], sem)

    def pass_load(x, side, u):
        p = u - (AHEAD if x == 3 else 0)
        at = (0, 2, 3, 1)[x] * owned + (core if side == 0 else 1 - core) * rows
        return load(x, side, p, u % 2, at, load_sem.at[x, side])

    def tail_load(i, side):
        at = i * owned + (core if side == 0 else 1 - core) * rows
        return load(3, side, tail_first + i, pieces % 2, at, load_sem.at[i, side])

    def split_queries(halves, slot, first, size, m):
        def body(j, c):
            col = pl.ds(pl.multiple_of(j * strip, strip), strip)
            scale = table_ref[ids_ref[(co * width + j * strip) // PROJ]]
            x = stage[slot, first:first + size, col] * scale
            hi = x.astype(jnp.bfloat16)
            halves[first:first + size, col] = hi
            halves[m + first:m + first + size, col] = (x - hi.astype(jnp.float32)).astype(jnp.bfloat16)
            return c

        lax.fori_loop(0, width // strip, body, 0)

    def scores(halves, m, b):
        cols = block_cols(b)
        both = jnp.dot(halves[:2 * m, :], ghi[:, cols], preferred_element_type=jnp.float32)
        small = both[m:] + jnp.dot(halves[:m, :], glo[:, cols], preferred_element_type=jnp.float32)
        return small + both[:m]

    def settle(total):
        squares = sq_own[...]
        for k in range(1, n_co):
            squares = squares + sq_got[k - 1]
        total = total * lax.rsqrt(squares[0:1] + epsilon)
        m = total.shape[0]
        hi = total.astype(jnp.bfloat16)
        rest = total - hi.astype(jnp.float32)
        half = rest.astype(jnp.bfloat16)
        last = (rest - half.astype(jnp.float32)).astype(jnp.bfloat16)
        three = jnp.concatenate([hi, half, last], axis=0)
        moved = jnp.dot(three, place[...], preferred_element_type=jnp.float32)
        return moved[:m] + (moved[m:2 * m] + moved[2 * m:])

    def out_copy(i, p):
        at = pl.ds(pl.multiple_of(i * pieces * rows + p * rows, rows), rows)
        return pltpu.make_async_copy(out_ref.at[at], final_ref.at[at], out_sem.at[i, p])

    def finish(u):
        for k in range(1, n_co):
            for b in range(blocks):
                part_copy(k, u, b).wait_recv()
        lag = (co == diag).astype(jnp.int32) * AHEAD
        first = u - lag

        @pl.when(first >= 0)
        def _():
            total = part[u, band(co)]
            for k in range(1, n_co):
                total = total + got[k - 1, u]
            moved = settle(total)
            for i in range(2):
                at = pl.multiple_of(i * pieces * rows + first * rows, rows)
                out_ref[pl.ds(at, rows), :] = moved[i * rows:(i + 1) * rows]
                out_copy(i, first).start()

    def early_own(u):
        pass_load(0, 0, u).start()

        @pl.when(u >= AHEAD)
        def _():
            share_diag(u - AHEAD)
            pass_load(3, 0, u).start()

    def early_sibling(u):
        sib_copy(0, u, True).wait_recv()
        pass_load(0, 1, u).start()

        @pl.when(u >= AHEAD)
        def _():
            sib_copy(3, u - AHEAD, True).wait_recv()
            pass_load(3, 1, u).start()

    early_own(0)
    early_sibling(0)

    def one_pass(u, c):
        for side in range(2):
            pass_load(0, side, u).wait()

        @pl.when(u >= AHEAD)
        def _():
            for side in range(2):
                pass_load(3, side, u).wait()

        split_queries(split, u % 2, 0, early, count)

        @pl.when(u > 1)
        def _():
            forward(u)

        for x in (2, 1):
            pass_load(x, 0, u).start()
        for x in (2, 1):
            sib_copy(x, u, True).wait_recv()
            pass_load(x, 1, u).start()
        for x in (2, 1):
            for side in range(2):
                pass_load(x, side, u).wait()
            split_queries(split, u % 2, early + (x - 1) * owned, owned, count)

        def score_block(b, c):
            part[u, :, block_cols(b)] = scores(split, count, b)
            for k in range(1, n_co):
                part_copy(k, u, b).start()

            @pl.when((u == 0) & (b == 0))
            def _():
                forward(1)

            @pl.when((u < pieces - 1) & (b == 1))
            def _():
                early_own(u + 1)

            @pl.when((u < pieces - 1) & (b == 2))
            def _():
                early_sibling(u + 1)

            @pl.when((u == pieces - 1) & (b == 1))
            def _():
                share_diag(tail_first)
                tail_load(0, 0).start()

            @pl.when((u == pieces - 1) & (b == 2))
            def _():
                sib_copy(3, tail_first, True).wait_recv()
                tail_load(0, 1).start()
                share_diag(tail_first + 1)
                tail_load(1, 0).start()

            return c

        lax.fori_loop(0, blocks, score_block, 0)

        @pl.when(u == 1)
        def _():
            for k in range(1, n_co):
                sq_copy(k).wait_recv()

        @pl.when((u > 0) & (u < pieces - 1))
        def _():
            finish(u - 1)

        return c

    lax.fori_loop(0, pieces, one_pass, 0)

    sib_copy(3, tail_first + 1, True).wait_recv()
    tail_load(1, 1).start()
    for i in range(AHEAD):
        tail_load(i, 0).wait()
        tail_load(i, 1).wait()
        split_queries(tail_split, pieces % 2, i * owned, owned, tail_rows)

    def tail_block(b, c):
        @pl.when(b < blocks)
        def _():
            tail_part[:, block_cols(b)] = scores(tail_split, tail_rows, b)

        ready = b - depth

        @pl.when((co != diag) & (ready >= 0) & (ready < blocks))
        def _():
            cols = block_cols(ready)
            for g in range(grains):
                @pl.when(depth > 0)
                def _():
                    tail_copy(above, ready, g).wait_recv()
                    tail_part[grain(g), cols] = tail_part[grain(g), cols] + tail_got[above, grain(g), cols]

                tail_copy(above, ready, g).start()

        return c

    lax.fori_loop(0, blocks + n_co - 2, tail_block, 0)
    finish(pieces - 2)
    finish(pieces - 1)

    @pl.when(co == diag)
    def _():
        def gather_side(slot):
            for b in range(blocks):
                for g in range(grains):
                    tail_copy(slot, b, g).wait_recv()
            tail_part[...] = tail_part[...] + tail_got[slot]

        @pl.when(co > 0)
        def _():
            gather_side(0)

        @pl.when(co < n_co - 1)
        def _():
            gather_side(1)

        moved = settle(tail_part[...])
        for i in range(AHEAD):
            for j in range(2):
                at = j * pieces * rows + (tail_first + i) * rows
                row = i * owned + j * rows
                out_ref[at:at + rows, :] = moved[row:row + rows]
                out_copy(j, tail_first + i).start()

    @pl.when(co != diag)
    def _():
        for b in range(blocks):
            for g in range(grains):
                tail_copy(above, b, g).wait_send()

    def drain(p, c):
        for way in range(2):
            own_copy(way, p, False).wait_send()
            relay_copy(way, p, False).wait_send()
        for x in range(4):
            sib_copy(x, p, False).wait_send()
        return c

    lax.fori_loop(0, pieces, drain, 0)

    def drain_parts(u, c):
        for k in range(1, n_co):
            for b in range(blocks):
                part_copy(k, u, b).wait_send()
        return c

    lax.fori_loop(0, pieces, drain_parts, 0)

    def drain_out(p, c):
        for i in range(2):
            out_copy(i, p).wait()
        return c

    lax.fori_loop(0, pieces, drain_out, 0)
    for k in range(1, n_co):
        sq_copy(k).wait_send()


MOVES = 4


def move_out(src, dst, box, in_sem, out_sem):
    size = src.shape[0] // MOVES

    def copy(a, b, sem, j):
        at = pl.ds(j * size, size)
        return pltpu.make_async_copy(a.at[at], b.at[at], sem.at[j])

    for j in range(MOVES):
        copy(src, box, in_sem, j).start()
    for j in range(MOVES):
        copy(src, box, in_sem, j).wait()
        copy(box, dst, out_sem, j).start()
    for j in range(MOVES):
        copy(box, dst, out_sem, j).wait()


def plane_shards(n_ex, n_co, train_grads, queries, module_ids, module_scale, example_ids):
    examples, width = train_grads.shape
    pieces = queries.shape[0] // UNIT
    count = n_ex * UNIT
    owned = 2 * UNIT
    tail_rows = 2 * AHEAD * UNIT
    f32, bf16 = jnp.float32, jnp.bfloat16
    dma = pltpu.SemaphoreType.DMA
    hbm = pl.BlockSpec(memory_space=pl.ANY)
    scores, _ = pl.pallas_call(
        functools.partial(plane_kernel, n_ex, n_co),
        out_shape=(
            jax.ShapeDtypeStruct((2 * queries.shape[0], examples), f32),
            jax.ShapeDtypeStruct((pieces, n_ex, UNIT, width), f32),
        ),
        in_specs=[hbm, hbm, hbm, hbm, hbm],
        out_specs=(hbm, hbm),
        scratch_shapes=[
            pltpu.SMEM(module_ids.shape, jnp.int32),
            pltpu.SMEM(module_scale.shape, f32),
            pltpu.VMEM((1, examples), jnp.int32),
            dma((3,)),
            pltpu.VMEM((2 * queries.shape[0], examples), f32),
            dma((2, pieces)),
            pltpu.VMEM((width, examples), bf16),
            pltpu.VMEM((width, examples), bf16),
            pltpu.VMEM((2, 128, width), f32),
            pltpu.VMEM((2 * count, width), bf16),
            pltpu.VMEM((2 * tail_rows, width), bf16),
            pltpu.VMEM((pieces, count, examples), f32),
            pltpu.VMEM((n_co - 1, pieces, owned, examples), f32),
            pltpu.VMEM((tail_rows, examples), f32),
            pltpu.VMEM((2, tail_rows, examples), f32),
            pltpu.VMEM((examples, examples), bf16),
            pltpu.VMEM((8, examples), f32),
            pltpu.VMEM((n_co - 1, 8, examples), f32),
            dma((2, pieces)),
            dma((2, pieces)),
            dma((2, pieces)),
            dma((2, pieces)),
            dma((4, pieces)),
            dma((4, pieces)),
            dma((n_co - 1, pieces, examples // 256)),
            dma((n_co - 1, pieces, examples // 256)),
            dma((examples // 256, 2 * AHEAD)),
            dma((2, examples // 256, 2 * AHEAD)),
            dma((n_co - 1,)),
            dma((n_co - 1,)),
            dma((4, 2)),
            dma((2,)),
        ],
        compiler_params=pltpu.CompilerParams(
            collective_id=0, has_side_effects=True, vmem_limit_bytes=67043328
        ),
    )(module_ids, module_scale, queries, train_grads, example_ids[None, :])
    return pl.pallas_call(
        move_out,
        out_shape=jax.ShapeDtypeStruct(scores.shape, f32),
        in_specs=[hbm],
        out_specs=hbm,
        scratch_shapes=[pltpu.VMEM(scores.shape, f32), dma((MOVES,)), dma((MOVES,))],
    )(scores)


def solution(mesh):
    n_ex, n_co = mesh.shape["ex"], mesh.shape["co"]
    body = plane_shards if n_ex == 8 and n_ex == 2 * n_co else shards
    return jax.shard_map(
        functools.partial(body, n_ex, n_co),
        mesh=mesh,
        in_specs=(P("ex", "co"), P("ex", "co"), P(), P(), P("ex")),
        out_specs=P("co", "ex"),
        check_vma=False,
    )
```
